32 devices in a mesh: band: 8 (over z, x), grid: 4 (over y, core).
Axes of the slice: x: 2, y: 2, z: 4, core: 2. Of those that a mesh axis runs over, the one named last changes fastest.
Arguments:
- bands: float32 [16, 96, 96, 96], P('band', 'grid'), may hold values from -6 to 6
Outputs:
- exchange_out: float32 [16, 96, 96, 96], P('band', 'grid')
The draws below stay inside these ranges and needn't reach their ends.
All inputs are finite; a program needn't handle non-finite values.
Results may differ from the reference program's by a relative error of at most 0.0091.
Values may be sent and summed in bfloat16 or wider, within the bound.
A program may use at most 128 MiB of HBM per device.

```python
import jax
import jax.numpy as jnp
import numpy as np
from jax import lax

NG = 96
BD = 2
ROUNDS = 3
BLOCKS = 8
NBANDS = 16


def shard_levels(stream_key, extent, split, least, largest):
    level, own = 1.0, jax.random.fold_in(stream_key, 6)
    for dim, parts in split:
        draws = jnp.exp(jax.random.uniform(jax.random.fold_in(own, dim), (parts,), jnp.float32, least / len(split), largest / len(split)))
        level = level * jnp.repeat(draws, extent[dim] // parts).reshape([-1 if axis == dim else 1 for axis in range(len(extent))])
    return level


def bell_draw(own_key, dims, width, reach, split=(), kind=jnp.bfloat16):
    array = width * jax.random.normal(own_key, dims, jnp.float32)
    if split:
        array = array * shard_levels(own_key, dims, split, -0.22, 0.18)
    return jnp.clip(array, -reach, reach).astype(kind)


def setup_inputs(seed: int = 0) -> dict:
    keys = jax.random.split(jax.random.key(seed), 2)
    return {
        "bands": bell_draw(keys[0], (NBANDS, NG, NG, NG), 1.0, 6.0, ((0, 8), (1, 4)), jnp.float32),
    }


kernel_scale = 16.0
screen_sq = 0.05


def dft_table(length):
    half = length // 2
    rows = np.arange(length)
    freq = np.where(rows <= half, rows, rows - half)
    phase = 2.0 * np.pi * np.outer(freq, rows) / length
    return np.where((rows <= half)[:, None], np.cos(phase), np.sin(phase))


def frequency_weights(rows, length):
    half = length // 2
    freq = jnp.where(rows <= half, rows, rows - half).astype(jnp.float32)
    weight = jnp.where((rows == 0) | (rows == half), 1.0, 2.0).astype(jnp.float32) / length
    return freq, weight


def multiplier(rows_x, rows_y, rows_z, length):
    freq_x, weight_x = frequency_weights(rows_x, length)
    freq_y, weight_y = frequency_weights(rows_y, length)
    freq_z, weight_z = frequency_weights(rows_z, length)
    square = freq_x[:, None, None] ** 2 + freq_y[None, :, None] ** 2 + freq_z[None, None, :] ** 2
    scale = weight_x[:, None, None] * weight_y[None, :, None] * weight_z[None, None, :]
    return kernel_scale * scale / (square + screen_sq)


def apply_table(form, cosines, data):
    return jnp.einsum(form, cosines.astype(jnp.float32), data.astype(jnp.float32), precision=lax.Precision.HIGHEST)


def potential_of(density, cosines, weights):
    section_one = apply_table("cz,pxyz->pxyc", cosines, density).astype(jnp.bfloat16)
    section_two = apply_table("cy,pxyz->pxcz", cosines, section_one).astype(jnp.bfloat16)
    section_three = (weights[None] * apply_table("cx,pxyz->pcyz", cosines, section_two)).astype(jnp.bfloat16)
    section_four = apply_table("cx,pcyz->pxyz", cosines, section_three).astype(jnp.bfloat16)
    section_five = apply_table("cy,pxcz->pxyz", cosines, section_four).astype(jnp.bfloat16)
    return apply_table("cz,pxyc->pxyz", cosines, section_five).astype(jnp.bfloat16)


def reference(bands):
    length = bands.shape[1]
    copies = bands.astype(jnp.bfloat16).reshape(BLOCKS, BD, length, length, length)
    cosines = jnp.asarray(dft_table(length), jnp.bfloat16)
    indices = jnp.arange(length, dtype=jnp.int32)
    weights = multiplier(indices, indices, indices, length)
    summed = jnp.zeros((BLOCKS, BD, length, length, length), jnp.float32)
    for round_index in range(1, ROUNDS + 1):
        partners = jnp.roll(copies, round_index, axis=0)

        def one_block(pair_blocks):
            mine, other = pair_blocks
            density = (mine[:, None].astype(jnp.float32) * other[None].astype(jnp.float32)).astype(jnp.bfloat16)
            density = density.reshape(BD * BD, length, length, length)
            field = potential_of(density, cosines, weights).reshape(BD, BD, length, length, length)
            own = jnp.einsum("ijxyz,jxyz->ixyz", field.astype(jnp.float32), other.astype(jnp.float32), precision=lax.Precision.HIGHEST)
            given = jnp.einsum("ijxyz,ixyz->jxyz", field.astype(jnp.float32), mine.astype(jnp.float32), precision=lax.Precision.HIGHEST)
            return own, given.astype(jnp.bfloat16)

        own, given = lax.map(one_block, (copies, partners))
        summed = summed + own + jnp.roll(given, -round_index, axis=0).astype(jnp.float32)
    return (-summed).reshape(bands.shape)
```

```python
import functools

import jax
import jax.numpy as jnp
import numpy as np
from jax import lax
from jax.experimental import pallas as pl
from jax.experimental.pallas import tpu as pltpu
from jax.sharding import PartitionSpec as P

kernel_scale = 16.0
screen_sq = 0.05

LANES = 128
GRID = 4
A0, A1, B0, B1, C = 0, 1, 2, 3, 4
MESH = pl.DeviceIdType.MESH
PITCH = 56
FWD, MID, BWD = 8, 16, 12
STEPS = ((B0, C), (A0, C), (A0, B0), (A1, B1), (A1, C), (B1, C))


def dft_table(length):
    half = length // 2
    rows = np.arange(length)
    freq = np.where(rows <= half, rows, rows - half)
    phase = 2.0 * np.pi * np.outer(freq, rows) / length
    return np.where((rows <= half)[:, None], np.cos(phase), np.sin(phase))


def dot(a, b):
    return jnp.dot(a, b, preferred_element_type=jnp.float32)


def kernel(n_blocks, length, planes, own_ref, fz_ref, iz_ref, r_ref, rt_ref, out_ref,
           rbuf, fbuf, bbuf, mult, acc, sendbuf, retbuf, presum,
           in_send, in_recv, out_send, out_recv, f_send, f_recv, b_send, b_recv, local_sem):
    half = length // 2
    packed = own_ref.shape[1]
    tails = planes - packed
    me = lax.axis_index("band")
    g = lax.axis_index("grid")
    y, c = lax.div(g, 2), lax.rem(g, 2)
    mate = 2 * y + (1 - c)
    across = 2 * (1 - y) + c
    side = (y, 1 - y)

    def block(offset):
        return lax.rem(me + offset + n_blocks, n_blocks)

    barrier = pltpu.get_barrier_semaphore()
    peers = [(me, mate), (me, across)] + [(block(o), g) for o in (-2, -1, 1, 2)]
    for peer in peers:
        pl.semaphore_signal(barrier, inc=1, device_id=peer, device_id_type=MESH)

    rows = lax.broadcasted_iota(jnp.int32, (length, LANES), 0)
    lane = lax.broadcasted_iota(jnp.int32, (length, LANES), 1)

    def freq_of(i):
        return jnp.where(i <= half, i, i - half).astype(jnp.float32)

    def weight_of(i):
        return jnp.where((i == 0) | (i == half), 1.0, 2.0).astype(jnp.float32) / length

    square_ac = freq_of(rows) ** 2 + freq_of(lane) ** 2 + screen_sq
    weight_ac = weight_of(rows) * weight_of(lane) * kernel_scale

    def fill(b, _):
        bb = jnp.full((length, LANES), c * half + b, jnp.int32)
        mult[b] = weight_ac * weight_of(bb) / (square_ac + freq_of(bb) ** 2)
        return 0

    pl.semaphore_wait(barrier, len(peers))

    def remote(src, dst, sends, recvs, index, to):
        return pltpu.make_async_remote_copy(
            src_ref=src, dst_ref=dst, send_sem=sends.at[index], recv_sem=recvs.at[index],
            device_id=to, device_id_type=MESH)

    def slab(slot, h):
        return rbuf.at[slot, h, pl.ds(0, packed)]

    def copy_in(slot, d):
        if slot in (A0, A1):
            if d == 0:
                return remote(own_ref.at[slot], slab(slot, y), in_send, in_recv, 2 * slot, (block(-1), g))
            return remote(slab(slot, y), slab(slot, y), in_send, in_recv, 2 * slot + 1, (me, across))
        if slot in (B0, B1):
            band = 1 - y if slot == B0 else y
            return remote(own_ref.at[band], slab(slot, y), in_send, in_recv, 2 * slot + 1, (me, across))
        if d == 0:
            return remote(own_ref.at[y], slab(C, y), in_send, in_recv, 2 * C, (block(2), g))
        return remote(slab(B0, 1 - y), slab(C, 1 - y), in_send, in_recv, 2 * C + 1, (block(2), g))

    local = [pltpu.make_async_copy(own_ref.at[side[i]], slab(B0 + i, y), local_sem.at[i]) for i in range(2)]
    for i in range(2):
        local[i].start()
    for slot, d in ((B0, 1), (C, 0), (A0, 0), (B1, 1), (A1, 0)):
        copy_in(slot, d).start()

    lax.fori_loop(0, half, fill, 0)

    def arrive(slot, d):
        if slot in (B0, B1) and d == 0:
            local[slot - B0].wait()
        else:
            copy_in(slot, d).wait_recv()
        if (slot, d) == (B0, 1):
            copy_in(C, 1).start()
        if slot in (A0, A1) and d == 0:
            copy_in(slot, 1).start()
        h = side[d]

        def unpack(q, _):
            p0 = pltpu.roll(rbuf[slot, h, q].astype(jnp.float32), 32, 1)
            p1 = pltpu.roll(rbuf[slot, h, tails + q].astype(jnp.float32), 64, 1)
            p2 = pltpu.roll(rbuf[slot, h, 2 * tails + q].astype(jnp.float32), 96, 1)
            tail = jnp.where(lane < 32, p0, jnp.where(lane < 64, p1, p2))
            rbuf[slot, h, packed + q] = tail.astype(jnp.bfloat16)
            return 0

        lax.fori_loop(0, tails, unpack, 0)

    def row(par, hh, x):
        return pl.multiple_of(((2 * par + hh) * length + x) * PITCH, 8)

    def base(d, core):
        return side[d] * half + core * planes

    def swap(n, d, buf, hh, core, sends, recvs):
        part = buf.at[pl.ds(row(n % 2, hh, base(d, core)), planes * PITCH)]
        return remote(part, part, sends, recvs, 2 * (n % 2) + d, (me, mate))

    def f_swap(n, d):
        return swap(n, d, fbuf, 1 - c, c, f_send, f_recv)

    def b_swap(n, d):
        return swap(n, d, bbuf, c, 1 - c, b_send, b_recv)

    def forward(n, d):
        one, two = STEPS[n]
        h = side[d]
        x0 = base(d, c)

        def body(it, _):
            for u in range(FWD // 2):
                p = it * FWD + 2 * u
                dens = []
                for v in range(2):
                    x = rbuf[one, h, p + v].astype(jnp.float32) * rbuf[two, h, p + v].astype(jnp.float32)
                    dens.append(x.astype(jnp.bfloat16))
                s1 = dot(jnp.concatenate(dens, axis=1), fz_ref[...]).astype(jnp.bfloat16)
                s2 = dot(r_ref[...], s1)
                for v in range(2):
                    for hh in range(2):
                        fbuf[pl.ds(row(n % 2, hh, x0 + p + v), half), :] = (
                            s2[hh * half:(hh + 1) * half, v * LANES:(v + 1) * LANES])
            return 0

        lax.fori_loop(0, planes // FWD, body, 0)
        f_swap(n, d).start()

    def middle(n):
        for d in range(2):
            f_swap(n, d).wait_recv()
        start = (2 * (n % 2) + c) * length * PITCH

        def body(it, _):
            for u in range(MID // 2):
                b = it * MID + 2 * u
                s2 = jnp.concatenate(
                    [fbuf[pl.ds(start + b + v, length, stride=PITCH), :].astype(jnp.bfloat16) for v in range(2)],
                    axis=1)
                m = jnp.concatenate([mult[b + v] for v in range(2)], axis=1)
                s3 = (m * dot(r_ref[...], s2)).astype(jnp.bfloat16)
                s4 = dot(rt_ref[...], s3)
                for v in range(2):
                    bbuf[pl.ds(start + b + v, length, stride=PITCH), :] = s4[:, v * LANES:(v + 1) * LANES]
            return 0

        lax.fori_loop(0, half // MID, body, 0)
        for d in (1, 0):
            b_swap(n, d).start()

    def backward(n, d):
        one, two = STEPS[n]
        new = {slot: all(slot not in step for step in STEPS[:n]) for slot in (one, two)}
        h = side[d]
        x0 = base(d, c)
        b_swap(n, d).wait_recv()

        def body(it, _):
            for u in range(BWD // 2):
                p = it * BWD + 2 * u
                s4 = []
                for v in range(2):
                    s4.append(jnp.concatenate(
                        [bbuf[pl.ds(row(n % 2, hh, x0 + p + v), half), :].astype(jnp.bfloat16) for hh in range(2)],
                        axis=0))
                s5 = dot(rt_ref[...], jnp.concatenate(s4, axis=1)).astype(jnp.bfloat16)
                pot = dot(s5, iz_ref[...]).astype(jnp.bfloat16).astype(jnp.float32)
                for v in range(2):
                    field = pot[:, v * LANES:(v + 1) * LANES]
                    for slot, pair in ((one, two), (two, one)):
                        term = field * rbuf[pair, h, p + v].astype(jnp.float32)
                        if new[slot]:
                            acc[slot, h, p + v] = term
                        else:
                            acc[slot, h, p + v] += term
            return 0

        lax.fori_loop(0, planes // BWD, body, 0)

    def settle(n):
        for d in range(2):
            f_swap(n, d).wait_send()
            b_swap(n, d).wait_send()

    def copy_out(slot, d):
        part = sendbuf.at[slot, side[d]]
        if slot in (A0, A1):
            if d == 1:
                return remote(part, presum.at[slot], out_send, out_recv, 2 * slot + 1, (me, across))
            return remote(part, retbuf.at[slot], out_send, out_recv, 2 * slot, (block(1), g))
        if slot in (B0, B1):
            band = y if slot == B0 else 1 - y
            return remote(part, retbuf.at[2 + band], out_send, out_recv, 2 * slot + 1, (me, across))
        if d == 1:
            return remote(part, presum.at[2], out_send, out_recv, 2 * C + 1, (block(-2), g))
        return remote(part, retbuf.at[4], out_send, out_recv, 2 * C, (block(-2), g))

    def mixed(slot, h, q, t):
        tail = acc[slot, h, packed + q]
        return jnp.where(lane < 96, acc[slot, h, t * tails + q], pltpu.roll(tail, 96 - 32 * t, 1))

    def leave(slot, d):
        h = side[d]
        extra = {(A0, 0): 0, (A1, 0): 1, (B0, 1): 2}.get((slot, d))
        if extra is not None:
            copy_out(*((C, 1) if slot == B0 else (slot, 1))).wait_recv()

        def pack(q, _):
            for t in range(3):
                value = mixed(slot, h, q, t)
                if extra is not None:
                    value = value + presum[extra, t * tails + q].astype(jnp.float32)
                sendbuf[slot, h, t * tails + q] = value.astype(jnp.bfloat16)
            return 0

        lax.fori_loop(0, tails, pack, 0)
        copy_out(slot, d).start()

    arrive(B0, 0)
    arrive(B0, 1)
    arrive(C, 0)
    forward(0, 0)
    arrive(A0, 0)
    arrive(C, 1)
    forward(0, 1)
    middle(0)
    arrive(A1, 0)
    arrive(A0, 1)
    for d in range(2):
        forward(1, d)
    for d in (1, 0):
        backward(0, d)
    settle(0)
    middle(1)
    for d in range(2):
        forward(2, d)
    for d in (1, 0):
        backward(1, d)
    settle(1)
    middle(2)
    for slot in (B1, A1):
        for d in range(2):
            if (slot, d) != (A1, 0):
                arrive(slot, d)
    for d in range(2):
        forward(3, d)
    backward(2, 1)
    leave(A0, 1)
    backward(2, 0)
    settle(2)
    middle(3)
    for d in range(2):
        forward(4, d)
    for d in (1, 0):
        backward(3, d)
    settle(3)
    leave(A0, 0)
    middle(4)
    for d in range(2):
        forward(5, d)
    backward(4, 1)
    leave(A1, 1)
    backward(4, 0)
    settle(4)
    middle(5)
    backward(5, 1)
    leave(C, 1)
    leave(B1, 1)
    backward(5, 0)
    leave(C, 0)
    settle(5)
    leave(A1, 0)
    leave(B0, 1)

    for slot in (B0, B1):
        copy_in(slot, 1).wait_send()
        copy_out(slot, 1).wait_send()
    for slot in (A0, A1, C):
        for d in range(2):
            copy_in(slot, d).wait_send()
            copy_out(slot, d).wait_send()
        copy_out(slot, 0).wait_recv()
    for slot in (B0, B1):
        copy_out(slot, 1).wait_recv()

    for i in range(2):
        band = side[i]

        def add(q, _):
            for t in range(3):
                p = t * tails + q
                total = mixed(B0 + i, y, q, t)
                total = total + retbuf[band, p].astype(jnp.float32)
                total = total + retbuf[2 + band, p].astype(jnp.float32)
                if i == 0:
                    total = total + retbuf[4, p].astype(jnp.float32)
                out_ref[band, p] = -total
            return 0

        lax.fori_loop(0, tails, add, 0)


def pack_planes(x, packed):
    tails = x.shape[1] - packed
    tail = x[:, packed:]
    side = jnp.concatenate([tail[..., 32 * t:32 * t + 32] for t in range(3)], axis=1)
    assert side.shape[1] == packed and tails * 3 == packed
    return jnp.concatenate([x[:, :packed], side], axis=-1)


def unpack_planes(x, length):
    packed = x.shape[1]
    tails = packed // 3
    side = x[..., length:]
    tail = jnp.concatenate([side[:, t * tails:(t + 1) * tails] for t in range(3)], axis=-1)
    return jnp.concatenate([x[..., :length], tail], axis=1)


def per_device(n_blocks, bands):
    count, planes, length, _ = bands.shape
    assert count == 2 and length == 96 and planes * GRID == length
    packed = planes * length // LANES
    table = dft_table(length)
    pad = np.zeros((LANES, LANES))
    pad[:length, :length] = table.T
    eye = np.eye(2)
    fz = jnp.asarray(np.kron(eye, pad), jnp.bfloat16)
    iz = jnp.asarray(np.kron(eye, pad.T), jnp.bfloat16)
    r = jnp.asarray(table, jnp.bfloat16)
    rt = jnp.asarray(table.T, jnp.bfloat16)
    own = pack_planes(bands.astype(jnp.bfloat16), packed)
    vmem = pl.BlockSpec(memory_space=pltpu.VMEM)
    out = pl.pallas_call(
        functools.partial(kernel, n_blocks, length, planes),
        out_shape=jax.ShapeDtypeStruct((count, packed, length, LANES), jnp.float32),
        in_specs=[vmem] * 5,
        out_specs=vmem,
        scratch_shapes=[
            pltpu.VMEM((5, 2, planes, length, LANES), jnp.bfloat16),
            pltpu.VMEM((4 * length * PITCH, LANES), jnp.float32),
            pltpu.VMEM((4 * length * PITCH, LANES), jnp.float32),
            pltpu.VMEM((length // 2, length, LANES), jnp.float32),
            pltpu.VMEM((5, 2, planes, length, LANES), jnp.float32),
            pltpu.VMEM((5, 2, packed, length, LANES), jnp.bfloat16),
            pltpu.VMEM((5, packed, length, LANES), jnp.bfloat16),
            pltpu.VMEM((3, packed, length, LANES), jnp.bfloat16),
            pltpu.SemaphoreType.DMA((10,)),
            pltpu.SemaphoreType.DMA((10,)),
            pltpu.SemaphoreType.DMA((10,)),
            pltpu.SemaphoreType.DMA((10,)),
            pltpu.SemaphoreType.DMA((4,)),
            pltpu.SemaphoreType.DMA((4,)),
            pltpu.SemaphoreType.DMA((4,)),
            pltpu.SemaphoreType.DMA((4,)),
            pltpu.SemaphoreType.DMA((2,)),
        ],
        compiler_params=pltpu.CompilerParams(
            collective_id=0, has_side_effects=True, vmem_limit_bytes=60000 * 1024),
    )(own, fz, iz, r, rt)
    return unpack_planes(out, length)


def solution(mesh):
    n_blocks = mesh.shape["band"]
    assert mesh.shape["grid"] == GRID
    in_specs = (P("band", "grid", None, None),)
    out_specs = P("band", "grid", None, None)
    return jax.shard_map(
        functools.partial(per_device, n_blocks), mesh=mesh, in_specs=in_specs, out_specs=out_specs,
        check_vma=False,
    )
```

```python
import functools

import jax
import jax.numpy as jnp
import numpy as np
from jax import lax
from jax.experimental import pallas as pl
from jax.experimental.pallas import tpu as pltpu
from jax.sharding import PartitionSpec as P

kernel_scale = 16.0
screen_sq = 0.05

LANES = 128
GRID = 4
A0, A1, B0, B1, C = 0, 1, 2, 3, 4
MESH = pl.DeviceIdType.MESH
PITCH = 56
RING = 4
FWD, MID, BWD = 8, 16, 12
STEPS = ((B0, C), (A0, C), (A0, B0), (A1, B1), (A1, C), (B1, C))


def dft_table(length):
    half = length // 2
    rows = np.arange(length)
    freq = np.where(rows <= half, rows, rows - half)
    phase = 2.0 * np.pi * np.outer(freq, rows) / length
    return np.where((rows <= half)[:, None], np.cos(phase), np.sin(phase))


def dot(a, b):
    return jnp.dot(a, b, preferred_element_type=jnp.float32)


def kernel(n_blocks, length, planes, own_ref, fz_ref, iz_ref, r_ref, rt_ref, out_ref,
           rbuf, main, aside, stage, mult, acc, sendbuf, retbuf, presum,
           in_send, in_recv, out_send, out_recv, f_send, f_recv, b_send, b_recv, local_sem):
    half = length // 2
    packed = own_ref.shape[1]
    tails = planes - packed
    me = lax.axis_index("band")
    g = lax.axis_index("grid")
    y, c = lax.div(g, 2), lax.rem(g, 2)
    mate = 2 * y + (1 - c)
    across = 2 * (1 - y) + c
    side = (y, 1 - y)

    def block(offset):
        return lax.rem(me + offset + n_blocks, n_blocks)

    barrier = pltpu.get_barrier_semaphore()
    peers = [(me, mate), (me, across)] + [(block(o), g) for o in (-2, -1, 1, 2)]
    for peer in peers:
        pl.semaphore_signal(barrier, inc=1, device_id=peer, device_id_type=MESH)

    rows = lax.broadcasted_iota(jnp.int32, (length, LANES), 0)
    lane = lax.broadcasted_iota(jnp.int32, (length, LANES), 1)

    def freq_of(i):
        return jnp.where(i <= half, i, i - half).astype(jnp.float32)

    def weight_of(i):
        return jnp.where((i == 0) | (i == half), 1.0, 2.0).astype(jnp.float32) / length

    square_ac = freq_of(rows) ** 2 + freq_of(lane) ** 2 + screen_sq
    weight_ac = weight_of(rows) * weight_of(lane) * kernel_scale

    def fill(b, _):
        bb = jnp.full((length, LANES), c * half + b, jnp.int32)
        mult[b] = weight_ac * weight_of(bb) / (square_ac + freq_of(bb) ** 2)
        return 0

    pl.semaphore_wait(barrier, len(peers))

    def remote(src, dst, sends, recvs, index, to):
        return pltpu.make_async_remote_copy(
            src_ref=src, dst_ref=dst, send_sem=sends.at[index], recv_sem=recvs.at[index],
            device_id=to, device_id_type=MESH)

    def slab(slot, h):
        return rbuf.at[slot, h, pl.ds(0, packed)]

    def copy_in(slot, d):
        if slot in (A0, A1):
            if d == 0:
                return remote(own_ref.at[slot], slab(slot, y), in_send, in_recv, 2 * slot, (block(-1), g))
            return remote(slab(slot, y), slab(slot, y), in_send, in_recv, 2 * slot + 1, (me, across))
        if slot in (B0, B1):
            band = 1 - y if slot == B0 else y
            return remote(own_ref.at[band], slab(slot, y), in_send, in_recv, 2 * slot + 1, (me, across))
        if d == 0:
            return remote(own_ref.at[y], slab(C, y), in_send, in_recv, 2 * C, (block(2), g))
        return remote(slab(B0, 1 - y), slab(C, 1 - y), in_send, in_recv, 2 * C + 1, (block(2), g))

    local = [pltpu.make_async_copy(own_ref.at[side[i]], slab(B0 + i, y), local_sem.at[i]) for i in range(2)]
    for i in range(2):
        local[i].start()
    for slot, d in ((B0, 1), (C, 0), (A0, 0), (B1, 1), (A1, 0)):
        copy_in(slot, d).start()

    lax.fori_loop(0, half, fill, 0)

    def arrive(slot, d):
        if slot in (B0, B1) and d == 0:
            local[slot - B0].wait()
        else:
            copy_in(slot, d).wait_recv()
        if (slot, d) == (B0, 1):
            copy_in(C, 1).start()
        if slot in (A0, A1) and d == 0:
            copy_in(slot, 1).start()
        h = side[d]

        def unpack(q, _):
            p0 = pltpu.roll(rbuf[slot, h, q].astype(jnp.float32), 32, 1)
            p1 = pltpu.roll(rbuf[slot, h, tails + q].astype(jnp.float32), 64, 1)
            p2 = pltpu.roll(rbuf[slot, h, 2 * tails + q].astype(jnp.float32), 96, 1)
            tail = jnp.where(lane < 32, p0, jnp.where(lane < 64, p1, p2))
            rbuf[slot, h, packed + q] = tail.astype(jnp.bfloat16)
            return 0

        lax.fori_loop(0, tails, unpack, 0)

    def main_row(n, x):
        return pl.multiple_of((n * length + x) * PITCH, 8)

    def aside_row(n, d, p):
        return pl.multiple_of((n * half + d * planes + p) * PITCH, 8)

    def base(d, core):
        return side[d] * half + core * planes

    def f_swap(n, d):
        return remote(stage.at[slot_of[n, d] % RING],
                      main.at[pl.ds(main_row(n, base(d, c)), planes * PITCH)],
                      f_send, f_recv, 2 * n + d, (me, mate))

    def b_swap(n, d):
        return remote(main.at[pl.ds(main_row(n, base(d, 1 - c)), planes * PITCH)],
                      aside.at[pl.ds(aside_row(n, d, 0), planes * PITCH)],
                      b_send, b_recv, 2 * n + d, (me, mate))

    slot_of = {}

    def forward(n, d):
        one, two = STEPS[n]
        slot_of[n, d] = len(slot_of)
        for key, slot in slot_of.items():
            if slot == slot_of[n, d] - RING:
                f_swap(*key).wait_send()
        h = side[d]
        x0 = base(d, c)

        def body(it, _):
            for u in range(FWD // 2):
                p = it * FWD + 2 * u
                dens = []
                for v in range(2):
                    x = rbuf[one, h, p + v].astype(jnp.float32) * rbuf[two, h, p + v].astype(jnp.float32)
                    dens.append(x.astype(jnp.bfloat16))
                s1 = dot(jnp.concatenate(dens, axis=1), fz_ref[...]).astype(jnp.bfloat16)
                s2 = dot(r_ref[...], s1)
                for v in range(2):
                    top, bottom = s2[:half, v * LANES:(v + 1) * LANES], s2[half:, v * LANES:(v + 1) * LANES]
                    main[pl.ds(main_row(n, x0 + p + v), half), :] = jnp.where(c == 0, top, bottom)
                    at = pl.multiple_of((p + v) * PITCH, 8)
                    stage[slot_of[n, d] % RING, pl.ds(at, half), :] = jnp.where(c == 0, bottom, top)
            return 0

        lax.fori_loop(0, planes // FWD, body, 0)
        f_swap(n, d).start()

    def middle(n):
        for d in range(2):
            f_swap(n, d).wait_recv()
        start = n * length * PITCH

        def body(it, _):
            for u in range(MID // 2):
                b = it * MID + 2 * u
                s2 = jnp.concatenate(
                    [main[pl.ds(start + b + v, length, stride=PITCH), :].astype(jnp.bfloat16) for v in range(2)],
                    axis=1)
                m = jnp.concatenate([mult[b + v] for v in range(2)], axis=1)
                s3 = (m * dot(r_ref[...], s2)).astype(jnp.bfloat16)
                s4 = dot(rt_ref[...], s3)
                for v in range(2):
                    main[pl.ds(start + b + v, length, stride=PITCH), :] = s4[:, v * LANES:(v + 1) * LANES]
            return 0

        lax.fori_loop(0, half // MID, body, 0)
        for d in (1, 0):
            b_swap(n, d).start()

    begun = set()

    def backward(n, d):
        one, two = STEPS[n]
        new = {slot: (slot, d) not in begun for slot in (one, two)}
        begun.update((slot, d) for slot in (one, two))
        h = side[d]
        x0 = base(d, c)
        b_swap(n, d).wait_recv()

        def body(it, _):
            for u in range(BWD // 2):
                p = it * BWD + 2 * u
                s4 = []
                for v in range(2):
                    mine = main[pl.ds(main_row(n, x0 + p + v), half), :].astype(jnp.bfloat16)
                    theirs = aside[pl.ds(aside_row(n, d, p + v), half), :].astype(jnp.bfloat16)
                    s4.append(jnp.concatenate([jnp.where(c == 0, mine, theirs), jnp.where(c == 0, theirs, mine)], axis=0))
                s5 = dot(rt_ref[...], jnp.concatenate(s4, axis=1)).astype(jnp.bfloat16)
                pot = dot(s5, iz_ref[...]).astype(jnp.bfloat16).astype(jnp.float32)
                for v in range(2):
                    field = pot[:, v * LANES:(v + 1) * LANES]
                    for slot, pair in ((one, two), (two, one)):
                        term = field * rbuf[pair, h, p + v].astype(jnp.float32)
                        if new[slot]:
                            acc[slot, h, p + v] = term
                        else:
                            acc[slot, h, p + v] += term
            return 0

        lax.fori_loop(0, planes // BWD, body, 0)

    def copy_out(slot, d):
        part = sendbuf.at[slot, side[d]]
        if slot in (A0, A1):
            if d == 1:
                return remote(part, presum.at[slot], out_send, out_recv, 2 * slot + 1, (me, across))
            return remote(part, retbuf.at[slot], out_send, out_recv, 2 * slot, (block(1), g))
        if slot in (B0, B1):
            band = y if slot == B0 else 1 - y
            return remote(part, retbuf.at[2 + band], out_send, out_recv, 2 * slot + 1, (me, across))
        if d == 1:
            return remote(part, presum.at[2], out_send, out_recv, 2 * C + 1, (block(-2), g))
        return remote(part, retbuf.at[4], out_send, out_recv, 2 * C, (block(-2), g))

    def mixed(slot, h, q, t):
        tail = acc[slot, h, packed + q]
        return jnp.where(lane < 96, acc[slot, h, t * tails + q], pltpu.roll(tail, 96 - 32 * t, 1))

    def leave(slot, d):
        h = side[d]
        extra = {(A0, 0): 0, (A1, 0): 1, (B0, 1): 2}.get((slot, d))
        if extra is not None:
            copy_out(*((C, 1) if slot == B0 else (slot, 1))).wait_recv()

        def pack(q, _):
            for t in range(3):
                value = mixed(slot, h, q, t)
                if extra is not None:
                    value = value + presum[extra, t * tails + q].astype(jnp.float32)
                sendbuf[slot, h, t * tails + q] = value.astype(jnp.bfloat16)
            return 0

        lax.fori_loop(0, tails, pack, 0)
        copy_out(slot, d).start()

    arrive(B0, 0)
    arrive(B1, 0)
    arrive(B0, 1)
    arrive(C, 0)
    forward(0, 0)
    forward(5, 0)
    arrive(A0, 0)
    forward(1, 0)
    forward(2, 0)
    arrive(C, 1)
    forward(0, 1)
    middle(0)
    arrive(A1, 0)
    arrive(B1, 1)
    forward(5, 1)
    backward(0, 1)
    middle(5)
    forward(3, 0)
    forward(4, 0)
    arrive(A0, 1)
    forward(1, 1)
    forward(2, 1)
    middle(1)
    middle(2)
    backward(1, 1)
    backward(2, 1)
    leave(A0, 1)
    arrive(A1, 1)
    forward(3, 1)
    forward(4, 1)
    middle(3)
    middle(4)
    backward(3, 1)
    backward(4, 1)
    leave(A1, 1)
    backward(5, 1)
    leave(C, 1)
    leave(B1, 1)
    backward(1, 0)
    backward(2, 0)
    leave(A0, 0)
    backward(0, 0)
    backward(4, 0)
    backward(5, 0)
    leave(C, 0)
    backward(3, 0)
    leave(A1, 0)
    leave(B0, 1)

    for n in range(len(STEPS)):
        for d in range(2):
            if slot_of[n, d] >= len(slot_of) - RING:
                f_swap(n, d).wait_send()
            b_swap(n, d).wait_send()
    for slot in (B0, B1):
        copy_in(slot, 1).wait_send()
        copy_out(slot, 1).wait_send()
    for slot in (A0, A1, C):
        for d in range(2):
            copy_in(slot, d).wait_send()
            copy_out(slot, d).wait_send()
        copy_out(slot, 0).wait_recv()
    for slot in (B0, B1):
        copy_out(slot, 1).wait_recv()

    for i in range(2):
        band = side[i]

        def add(q, _):
            for t in range(3):
                p = t * tails + q
                total = mixed(B0 + i, y, q, t)
                total = total + retbuf[band, p].astype(jnp.float32)
                total = total + retbuf[2 + band, p].astype(jnp.float32)
                if i == 0:
                    total = total + retbuf[4, p].astype(jnp.float32)
                out_ref[band, p] = -total
            return 0

        lax.fori_loop(0, tails, add, 0)


def pack_planes(x, packed):
    tails = x.shape[1] - packed
    tail = x[:, packed:]
    side = jnp.concatenate([tail[..., 32 * t:32 * t + 32] for t in range(3)], axis=1)
    assert side.shape[1] == packed and tails * 3 == packed
    return jnp.concatenate([x[:, :packed], side], axis=-1)


def unpack_planes(x, length):
    packed = x.shape[1]
    tails = packed // 3
    side = x[..., length:]
    tail = jnp.concatenate([side[:, t * tails:(t + 1) * tails] for t in range(3)], axis=-1)
    return jnp.concatenate([x[..., :length], tail], axis=1)


def per_device(n_blocks, bands):
    count, planes, length, _ = bands.shape
    assert count == 2 and length == 96 and planes * GRID == length
    packed = planes * length // LANES
    table = dft_table(length)
    pad = np.zeros((LANES, LANES))
    pad[:length, :length] = table.T
    eye = np.eye(2)
    fz = jnp.asarray(np.kron(eye, pad), jnp.bfloat16)
    iz = jnp.asarray(np.kron(eye, pad.T), jnp.bfloat16)
    r = jnp.asarray(table, jnp.bfloat16)
    rt = jnp.asarray(table.T, jnp.bfloat16)
    own = pack_planes(bands.astype(jnp.bfloat16), packed)
    vmem = pl.BlockSpec(memory_space=pltpu.VMEM)
    out = pl.pallas_call(
        functools.partial(kernel, n_blocks, length, planes),
        out_shape=jax.ShapeDtypeStruct((count, packed, length, LANES), jnp.float32),
        in_specs=[vmem] * 5,
        out_specs=vmem,
        scratch_shapes=[
            pltpu.VMEM((5, 2, planes, length, LANES), jnp.bfloat16),
            pltpu.VMEM((len(STEPS) * length * PITCH, LANES), jnp.float32),
            pltpu.VMEM((len(STEPS) * length // 2 * PITCH, LANES), jnp.float32),
            pltpu.VMEM((RING, planes * PITCH, LANES), jnp.float32),
            pltpu.VMEM((length // 2, length, LANES), jnp.float32),
            pltpu.VMEM((5, 2, planes, length, LANES), jnp.float32),
            pltpu.VMEM((5, 2, packed, length, LANES), jnp.bfloat16),
            pltpu.VMEM((5, packed, length, LANES), jnp.bfloat16),
            pltpu.VMEM((3, packed, length, LANES), jnp.bfloat16),
            pltpu.SemaphoreType.DMA((10,)),
            pltpu.SemaphoreType.DMA((10,)),
            pltpu.SemaphoreType.DMA((10,)),
            pltpu.SemaphoreType.DMA((10,)),
            pltpu.SemaphoreType.DMA((2 * len(STEPS),)),
            pltpu.SemaphoreType.DMA((2 * len(STEPS),)),
            pltpu.SemaphoreType.DMA((2 * len(STEPS),)),
            pltpu.SemaphoreType.DMA((2 * len(STEPS),)),
            pltpu.SemaphoreType.DMA((2,)),
        ],
        compiler_params=pltpu.CompilerParams(
            collective_id=0, has_side_effects=True, vmem_limit_bytes=60000 * 1024),
    )(own, fz, iz, r, rt)
    return unpack_planes(out, length)


def solution(mesh):
    n_blocks = mesh.shape["band"]
    assert mesh.shape["grid"] == GRID
    in_specs = (P("band", "grid", None, None),)
    out_specs = P("band", "grid", None, None)
    return jax.shard_map(
        functools.partial(per_device, n_blocks), mesh=mesh, in_specs=in_specs, out_specs=out_specs,
        check_vma=False,
    )
```

```python
import functools

import jax
import jax.numpy as jnp
import numpy as np
from jax import lax
from jax.experimental import pallas as pl
from jax.experimental.pallas import tpu as pltpu
from jax.sharding import PartitionSpec as P

kernel_scale = 16.0
screen_sq = 0.05

LANES = 128
GRID = 4
A0, A1, B0, B1, C = 0, 1, 2, 3, 4
MESH = pl.DeviceIdType.MESH
PITCH = 56
RING = 4
FWD, MID, BWD = 8, 16, 12
STEPS = ((B0, C), (A0, C), (A0, B0), (A1, B1), (A1, C), (B1, C))


def dft_table(length):
    half = length // 2
    rows = np.arange(length)
    freq = np.where(rows <= half, rows, rows - half)
    phase = 2.0 * np.pi * np.outer(freq, rows) / length
    return np.where((rows <= half)[:, None], np.cos(phase), np.sin(phase))


def dot(a, b):
    return jnp.dot(a, b, preferred_element_type=jnp.float32)


def kernel(n_blocks, length, planes, bands_ref, fz_ref, iz_ref, r_ref, rt_ref, out_ref,
           own_ref, rbuf, main, aside, stage, mult, acc, sendbuf, retbuf, presum,
           in_send, in_recv, out_send, out_recv, f_send, f_recv, b_send, b_recv, local_sem):
    half = length // 2
    packed = own_ref.shape[1]
    tails = planes - packed
    me = lax.axis_index("band")
    g = lax.axis_index("grid")
    y, c = lax.div(g, 2), lax.rem(g, 2)
    mate = 2 * y + (1 - c)
    across = 2 * (1 - y) + c
    side = (y, 1 - y)

    def block(offset):
        return lax.rem(me + offset + n_blocks, n_blocks)

    barrier = pltpu.get_barrier_semaphore()
    peers = [(me, mate), (me, across)] + [(block(o), g) for o in (-2, -1, 1, 2)]
    for peer in peers:
        pl.semaphore_signal(barrier, inc=1, device_id=peer, device_id_type=MESH)

    rows = lax.broadcasted_iota(jnp.int32, (length, LANES), 0)
    lane = lax.broadcasted_iota(jnp.int32, (length, LANES), 1)

    def freq_of(i):
        return jnp.where(i <= half, i, i - half).astype(jnp.float32)

    def weight_of(i):
        return jnp.where((i == 0) | (i == half), 1.0, 2.0).astype(jnp.float32) / length

    square_ac = freq_of(rows) ** 2 + freq_of(lane) ** 2 + screen_sq
    weight_ac = weight_of(rows) * weight_of(lane) * kernel_scale

    def fill(b, _):
        bb = jnp.full((length, LANES), c * half + b, jnp.int32)
        mult[b] = weight_ac * weight_of(bb) / (square_ac + freq_of(bb) ** 2)
        return 0

    gap = jnp.zeros((length, LANES - length), jnp.float32)

    def shrink(q, _):
        for s in range(2):
            tail = jnp.concatenate([bands_ref[s, packed + q], gap], axis=1)
            for t in range(3):
                head = jnp.concatenate([bands_ref[s, t * tails + q], gap], axis=1)
                head = jnp.where(lane < length, head, pltpu.roll(tail, (length - 32 * t) % LANES, 1))
                own_ref[s, t * tails + q] = head.astype(jnp.bfloat16)
        return 0

    lax.fori_loop(0, tails, shrink, 0)
    pl.semaphore_wait(barrier, len(peers))

    def remote(src, dst, sends, recvs, index, to):
        return pltpu.make_async_remote_copy(
            src_ref=src, dst_ref=dst, send_sem=sends.at[index], recv_sem=recvs.at[index],
            device_id=to, device_id_type=MESH)

    def slab(slot, h):
        return rbuf.at[slot, h, pl.ds(0, packed)]

    def copy_in(slot, d):
        if slot in (A0, A1):
            if d == 0:
                return remote(own_ref.at[slot], slab(slot, y), in_send, in_recv, 2 * slot, (block(-1), g))
            return remote(slab(slot, y), slab(slot, y), in_send, in_recv, 2 * slot + 1, (me, across))
        if slot in (B0, B1):
            band = 1 - y if slot == B0 else y
            return remote(own_ref.at[band], slab(slot, y), in_send, in_recv, 2 * slot + 1, (me, across))
        if d == 0:
            return remote(own_ref.at[y], slab(C, y), in_send, in_recv, 2 * C, (block(2), g))
        return remote(slab(B0, 1 - y), slab(C, 1 - y), in_send, in_recv, 2 * C + 1, (block(2), g))

    local = [pltpu.make_async_copy(own_ref.at[side[i]], slab(B0 + i, y), local_sem.at[i]) for i in range(2)]
    for i in range(2):
        local[i].start()
    for slot, d in ((B0, 1), (C, 0), (A0, 0), (B1, 1), (A1, 0)):
        copy_in(slot, d).start()

    lax.fori_loop(0, half, fill, 0)

    def arrive(slot, d):
        if slot in (B0, B1) and d == 0:
            local[slot - B0].wait()
        else:
            copy_in(slot, d).wait_recv()
        if (slot, d) == (B0, 1):
            copy_in(C, 1).start()
        if slot in (A0, A1) and d == 0:
            copy_in(slot, 1).start()
        h = side[d]

        def unpack(q, _):
            p0 = pltpu.roll(rbuf[slot, h, q].astype(jnp.float32), 32, 1)
            p1 = pltpu.roll(rbuf[slot, h, tails + q].astype(jnp.float32), 64, 1)
            p2 = pltpu.roll(rbuf[slot, h, 2 * tails + q].astype(jnp.float32), 96, 1)
            tail = jnp.where(lane < 32, p0, jnp.where(lane < 64, p1, p2))
            rbuf[slot, h, packed + q] = tail.astype(jnp.bfloat16)
            return 0

        lax.fori_loop(0, tails, unpack, 0)

    def main_row(n, x):
        return pl.multiple_of((n * length + x) * PITCH, 8)

    def aside_row(n, d, p):
        return pl.multiple_of((n * half + d * planes + p) * PITCH, 8)

    def base(d, core):
        return side[d] * half + core * planes

    def f_swap(n, d):
        return remote(stage.at[slot_of[n, d] % RING],
                      main.at[pl.ds(main_row(n, base(d, c)), planes * PITCH)],
                      f_send, f_recv, 2 * n + d, (me, mate))

    def b_swap(n, d):
        return remote(main.at[pl.ds(main_row(n, base(d, 1 - c)), planes * PITCH)],
                      aside.at[pl.ds(aside_row(n, d, 0), planes * PITCH)],
                      b_send, b_recv, 2 * n + d, (me, mate))

    slot_of = {}

    def forward(n, d):
        one, two = STEPS[n]
        slot_of[n, d] = len(slot_of)
        for key, slot in slot_of.items():
            if slot == slot_of[n, d] - RING:
                f_swap(*key).wait_send()
        h = side[d]
        x0 = base(d, c)

        def body(it, _):
            for u in range(FWD // 2):
                p = it * FWD + 2 * u
                dens = []
                for v in range(2):
                    x = rbuf[one, h, p + v].astype(jnp.float32) * rbuf[two, h, p + v].astype(jnp.float32)
                    dens.append(x.astype(jnp.bfloat16))
                s1 = dot(jnp.concatenate(dens, axis=1), fz_ref[...]).astype(jnp.bfloat16)
                s2 = dot(r_ref[...], s1)
                for v in range(2):
                    top, bottom = s2[:half, v * LANES:(v + 1) * LANES], s2[half:, v * LANES:(v + 1) * LANES]
                    main[pl.ds(main_row(n, x0 + p + v), half), :] = jnp.where(c == 0, top, bottom)
                    at = pl.multiple_of((p + v) * PITCH, 8)
                    stage[slot_of[n, d] % RING, pl.ds(at, half), :] = jnp.where(c == 0, bottom, top)
            return 0

        lax.fori_loop(0, planes // FWD, body, 0)
        f_swap(n, d).start()

    def middle(n):
        for d in range(2):
            f_swap(n, d).wait_recv()
        start = n * length * PITCH

        def body(it, _):
            for u in range(MID // 2):
                b = it * MID + 2 * u
                s2 = jnp.concatenate(
                    [main[pl.ds(start + b + v, length, stride=PITCH), :].astype(jnp.bfloat16) for v in range(2)],
                    axis=1)
                m = jnp.concatenate([mult[b + v] for v in range(2)], axis=1)
                s3 = (m * dot(r_ref[...], s2)).astype(jnp.bfloat16)
                s4 = dot(rt_ref[...], s3)
                for v in range(2):
                    main[pl.ds(start + b + v, length, stride=PITCH), :] = s4[:, v * LANES:(v + 1) * LANES]
            return 0

        lax.fori_loop(0, half // MID, body, 0)
        for d in (1, 0):
            b_swap(n, d).start()

    begun = set()

    def backward(n, d):
        one, two = STEPS[n]
        new = {slot: (slot, d) not in begun for slot in (one, two)}
        begun.update((slot, d) for slot in (one, two))
        h = side[d]
        x0 = base(d, c)
        b_swap(n, d).wait_recv()

        def body(it, _):
            for u in range(BWD // 2):
                p = it * BWD + 2 * u
                s4 = []
                for v in range(2):
                    mine = main[pl.ds(main_row(n, x0 + p + v), half), :].astype(jnp.bfloat16)
                    theirs = aside[pl.ds(aside_row(n, d, p + v), half), :].astype(jnp.bfloat16)
                    s4.append(jnp.concatenate([jnp.where(c == 0, mine, theirs), jnp.where(c == 0, theirs, mine)], axis=0))
                s5 = dot(rt_ref[...], jnp.concatenate(s4, axis=1)).astype(jnp.bfloat16)
                pot = dot(s5, iz_ref[...]).astype(jnp.bfloat16).astype(jnp.float32)
                for v in range(2):
                    field = pot[:, v * LANES:(v + 1) * LANES]
                    for slot, pair in ((one, two), (two, one)):
                        term = field * rbuf[pair, h, p + v].astype(jnp.float32)
                        if new[slot]:
                            acc[slot, h, p + v] = term
                        else:
                            acc[slot, h, p + v] += term
            return 0

        lax.fori_loop(0, planes // BWD, body, 0)

    def copy_out(slot, d):
        part = sendbuf.at[slot, side[d]]
        if slot in (A0, A1):
            if d == 1:
                return remote(part, presum.at[slot], out_send, out_recv, 2 * slot + 1, (me, across))
            return remote(part, retbuf.at[slot], out_send, out_recv, 2 * slot, (block(1), g))
        if slot in (B0, B1):
            band = y if slot == B0 else 1 - y
            return remote(part, retbuf.at[2 + band], out_send, out_recv, 2 * slot + 1, (me, across))
        if d == 1:
            return remote(part, presum.at[2], out_send, out_recv, 2 * C + 1, (block(-2), g))
        return remote(part, retbuf.at[4], out_send, out_recv, 2 * C, (block(-2), g))

    def mixed(slot, h, q, t):
        tail = acc[slot, h, packed + q]
        return jnp.where(lane < 96, acc[slot, h, t * tails + q], pltpu.roll(tail, 96 - 32 * t, 1))

    def leave(slot, d):
        h = side[d]
        extra = {(A0, 0): 0, (A1, 0): 1, (B0, 1): 2}.get((slot, d))
        if extra is not None:
            copy_out(*((C, 1) if slot == B0 else (slot, 1))).wait_recv()

        def pack(q, _):
            for t in range(3):
                value = mixed(slot, h, q, t)
                if extra is not None:
                    value = value + presum[extra, t * tails + q].astype(jnp.float32)
                sendbuf[slot, h, t * tails + q] = value.astype(jnp.bfloat16)
            return 0

        lax.fori_loop(0, tails, pack, 0)
        copy_out(slot, d).start()

    arrive(B0, 0)
    arrive(B1, 0)
    arrive(B0, 1)
    arrive(C, 0)
    forward(0, 0)
    forward(5, 0)
    arrive(A0, 0)
    forward(1, 0)
    forward(2, 0)
    arrive(C, 1)
    forward(0, 1)
    middle(0)
    arrive(A1, 0)
    arrive(B1, 1)
    forward(5, 1)
    backward(0, 1)
    middle(5)
    forward(3, 0)
    forward(4, 0)
    arrive(A0, 1)
    forward(1, 1)
    forward(2, 1)
    middle(1)
    middle(2)
    backward(1, 1)
    backward(2, 1)
    leave(A0, 1)
    arrive(A1, 1)
    forward(3, 1)
    forward(4, 1)
    middle(3)
    middle(4)
    backward(3, 1)
    backward(4, 1)
    leave(A1, 1)
    backward(5, 1)
    leave(C, 1)
    leave(B1, 1)
    backward(1, 0)
    backward(2, 0)
    leave(A0, 0)
    backward(0, 0)
    backward(4, 0)
    backward(5, 0)
    leave(C, 0)
    backward(3, 0)
    leave(A1, 0)
    leave(B0, 1)

    for n in range(len(STEPS)):
        for d in range(2):
            if slot_of[n, d] >= len(slot_of) - RING:
                f_swap(n, d).wait_send()
            b_swap(n, d).wait_send()
    for slot in (B0, B1):
        copy_in(slot, 1).wait_send()
        copy_out(slot, 1).wait_send()
    for slot in (A0, A1, C):
        for d in range(2):
            copy_in(slot, d).wait_send()
            copy_out(slot, d).wait_send()
        copy_out(slot, 0).wait_recv()
    for slot in (B0, B1):
        copy_out(slot, 1).wait_recv()

    for i in range(2):
        band = side[i]

        def add(q, _):
            for t in range(3):
                p = t * tails + q
                total = mixed(B0 + i, y, q, t)
                total = total + retbuf[band, p].astype(jnp.float32)
                total = total + retbuf[2 + band, p].astype(jnp.float32)
                if i == 0:
                    total = total + retbuf[4, p].astype(jnp.float32)
                out_ref[band, p] = -total
            return 0

        lax.fori_loop(0, tails, add, 0)


def unpack_planes(x, length):
    packed = x.shape[1]
    tails = packed // 3
    side = x[..., length:]
    tail = jnp.concatenate([side[:, t * tails:(t + 1) * tails] for t in range(3)], axis=-1)
    return jnp.concatenate([x[..., :length], tail], axis=1)


def per_device(n_blocks, bands):
    count, planes, length, _ = bands.shape
    assert count == 2 and length == 96 and planes * GRID == length
    packed = planes * length // LANES
    table = dft_table(length)
    pad = np.zeros((LANES, LANES))
    pad[:length, :length] = table.T
    eye = np.eye(2)
    fz = jnp.asarray(np.kron(eye, pad), jnp.bfloat16)
    iz = jnp.asarray(np.kron(eye, pad.T), jnp.bfloat16)
    r = jnp.asarray(table, jnp.bfloat16)
    rt = jnp.asarray(table.T, jnp.bfloat16)
    assert 4 * packed == 3 * planes
    vmem = pl.BlockSpec(memory_space=pltpu.VMEM)
    out = pl.pallas_call(
        functools.partial(kernel, n_blocks, length, planes),
        out_shape=jax.ShapeDtypeStruct((count, packed, length, LANES), jnp.float32),
        in_specs=[vmem] * 5,
        out_specs=vmem,
        scratch_shapes=[
            pltpu.VMEM((count, packed, length, LANES), jnp.bfloat16),
            pltpu.VMEM((5, 2, planes, length, LANES), jnp.bfloat16),
            pltpu.VMEM((len(STEPS) * length * PITCH, LANES), jnp.float32),
            pltpu.VMEM((len(STEPS) * length // 2 * PITCH, LANES), jnp.float32),
            pltpu.VMEM((RING, planes * PITCH, LANES), jnp.float32),
            pltpu.VMEM((length // 2, length, LANES), jnp.float32),
            pltpu.VMEM((5, 2, planes, length, LANES), jnp.float32),
            pltpu.VMEM((5, 2, packed, length, LANES), jnp.bfloat16),
            pltpu.VMEM((5, packed, length, LANES), jnp.bfloat16),
            pltpu.VMEM((3, packed, length, LANES), jnp.bfloat16),
            pltpu.SemaphoreType.DMA((10,)),
            pltpu.SemaphoreType.DMA((10,)),
            pltpu.SemaphoreType.DMA((10,)),
            pltpu.SemaphoreType.DMA((10,)),
            pltpu.SemaphoreType.DMA((2 * len(STEPS),)),
            pltpu.SemaphoreType.DMA((2 * len(STEPS),)),
            pltpu.SemaphoreType.DMA((2 * len(STEPS),)),
            pltpu.SemaphoreType.DMA((2 * len(STEPS),)),
            pltpu.SemaphoreType.DMA((2,)),
        ],
        compiler_params=pltpu.CompilerParams(
            collective_id=0, has_side_effects=True, vmem_limit_bytes=64000 * 1024),
    )(bands, fz, iz, r, rt)
    return unpack_planes(out, length)


def solution(mesh):
    n_blocks = mesh.shape["band"]
    assert mesh.shape["grid"] == GRID
    in_specs = (P("band", "grid", None, None),)
    out_specs = P("band", "grid", None, None)
    return jax.shard_map(
        functools.partial(per_device, n_blocks), mesh=mesh, in_specs=in_specs, out_specs=out_specs,
        check_vma=False,
    )
```
